32 devices in a mesh: layer: 4 (over y, x), row: 2 (over core), col: 4 (over z).
Axes of the slice: x: 2, y: 2, z: 4, core: 2. Of those that a mesh axis runs over, the one named last changes fastest.
Arguments:
- even_left: bfloat16 [2, 4, 32, 32, 256, 128], P(None, 'layer', 'row', 'col'), may hold values from -0.09375 to 0.09375
- even_right: bfloat16 [2, 4, 32, 32, 256, 128], P(None, 'layer', 'row', 'col'), may hold values from -0.25 to 0.25
- odd_left: bfloat16 [2, 4, 32, 32, 256, 128], P(None, 'layer', 'col', 'row'), may hold values from -0.09375 to 0.09375
- odd_right: bfloat16 [2, 4, 32, 32, 256, 128], P(None, 'layer', 'col', 'row'), may hold values from -0.25 to 0.25
- even_ranks: int32 [2, 4, 32, 32], P(None, 'layer', 'row', 'col'), may hold values from 16 to 64, as said below
- odd_ranks: int32 [2, 4, 32, 32], P(None, 'layer', 'col', 'row'), may hold values from 16 to 64, as said below
- even_sources: float32 [2, 4, 2, 8192, 128], P(None, 'layer', None, ('row', 'col')), may hold values from -6 to 6
- odd_sources: float32 [2, 4, 2, 8192, 128], P(None, 'layer', None, ('col', 'row')), may hold values from -6 to 6
Outputs:
- even_traces: float32 [4, 2, 8192, 128], P('layer', None, ('row', 'col'))
- odd_traces: float32 [4, 2, 8192, 128], P('layer', None, ('col', 'row'))
The draws below stay inside these ranges and needn't reach their ends.
Inputs may be any that keep to these rules, and one draw needn't show every extreme that they name: `even_ranks`: every direction and pair has a tile of rank 64 and a tile of rank a quarter of 64. `odd_ranks`: every direction and pair has a tile of rank 64 and a tile of rank a quarter of 64.
All inputs are finite; a program needn't handle non-finite values.
Results may differ from the reference program's by a relative error of at most 0.008.
Values may be sent and summed in bfloat16 or wider, within the bound.
A program may use at most 256 MiB of HBM per device.

```python
import jax
import jax.numpy as jnp
from jax import lax

NT = 8192
TILE = 256
RMAX = 64
BATCH = 64
NB = 2
TILES = 32
PAIRS = 4
LAYERS = 8


def rank_table(seed_key):
    total = TILES * TILES
    drawn = jax.random.randint(jax.random.fold_in(seed_key, 11), (2, PAIRS, total), RMAX // 4, RMAX + 1)
    top_spot = jax.random.randint(jax.random.fold_in(seed_key, 12), (2, PAIRS, 1), 0, total)
    offset = jax.random.randint(jax.random.fold_in(seed_key, 13), (2, PAIRS, 1), 0, total - 1)
    low_spot = (top_spot + 1 + offset) % total
    places = lax.iota(jnp.int32, total)[None, None, :]
    rank_grid = jnp.where(places == top_spot, RMAX, drawn)
    rank_grid = jnp.where(places == low_spot, RMAX // 4, rank_grid)
    return rank_grid.reshape(2, PAIRS, TILES, TILES).astype(jnp.int32)


def draw_even_ranks(key, part):
    return rank_table(jax.random.fold_in(key, 1))


def draw_odd_ranks(key, part):
    return rank_table(jax.random.fold_in(key, 2))


def shard_levels(key, shape, shards, low, high):
    level, own = 1.0, jax.random.fold_in(key, 6)
    for position, blocks in shards:
        steps = jnp.exp(jax.random.uniform(jax.random.fold_in(own, position), (blocks,), jnp.float32, low / len(shards), high / len(shards)))
        level = level * jnp.repeat(steps, shape[position] // blocks).reshape([-1 if axis == position else 1 for axis in range(len(shape))])
    return level


def centred(key, extent, scale, reach, cuts=(), dtype=jnp.bfloat16):
    array = jax.random.normal(key, extent, jnp.float32) * scale
    if len(cuts) > 0:
        array = shard_levels(key, extent, cuts, -0.22, 0.18) * array
    return jnp.clip(array, min=-reach, max=reach).astype(dtype)


def setup_inputs(seed: int = 0) -> dict:
    arg_keys = jax.random.split(jax.random.key(seed), 9)
    even_left = centred(arg_keys[0], (2, PAIRS, TILES, TILES, TILE, 2 * RMAX), (2 * RMAX * TILES) ** -0.5, 0.09375, ((1, 4), (2, 2), (3, 4)))
    even_right = centred(arg_keys[1], (2, PAIRS, TILES, TILES, TILE, 2 * RMAX), (2 * TILE) ** -0.5, 0.25, ((1, 4), (2, 2), (3, 4)))
    odd_left = centred(arg_keys[2], (2, PAIRS, TILES, TILES, TILE, 2 * RMAX), (2 * RMAX * TILES) ** -0.5, 0.09375, ((1, 4), (2, 4), (3, 2)))
    odd_right = centred(arg_keys[3], (2, PAIRS, TILES, TILES, TILE, 2 * RMAX), (2 * TILE) ** -0.5, 0.25, ((1, 4), (2, 4), (3, 2)))
    even_ranks = draw_even_ranks(jax.random.fold_in(arg_keys[8], 71), 0)
    odd_ranks = draw_odd_ranks(jax.random.fold_in(arg_keys[8], 71), 0)
    even_sources = centred(arg_keys[6], (2, PAIRS, NB, NT, 2 * BATCH), 1.0, 6.0, ((1, 4), (3, 8)), jnp.float32)
    odd_sources = centred(arg_keys[7], (2, PAIRS, NB, NT, 2 * BATCH), 1.0, 6.0, ((1, 4), (3, 8)), jnp.float32)
    return dict(even_left=even_left, even_right=even_right, odd_left=odd_left, odd_right=odd_right, even_ranks=even_ranks, odd_ranks=odd_ranks, even_sources=even_sources, odd_sources=odd_sources)


def tile_product(gathered, left_factor, right_factor, tile_ranks):
    batch_count = gathered.shape[0]
    tile_rows, tile_cols, tile_size, twice_rank = right_factor.shape
    half_rank = twice_rank // 2
    width = gathered.shape[2]
    half_cols = width // 2
    traces = gathered.reshape(batch_count, tile_cols, tile_size, width).astype(jnp.float32)
    products = jnp.einsum('acnr,kcnb->kacrb', right_factor.astype(jnp.float32), traces, preferred_element_type=jnp.float32)
    real_part = products[:, :, :, :half_rank, :half_cols] - products[:, :, :, half_rank:, half_cols:]
    imag_part = products[:, :, :, :half_rank, half_cols:] + products[:, :, :, half_rank:, :half_cols]
    rank_mask = (lax.iota(jnp.int32, half_rank)[None, None, :] < tile_ranks[:, :, None]).astype(jnp.float32)
    rank_mask = rank_mask[None, :, :, :, None]
    real_part = real_part * rank_mask
    imag_part = imag_part * rank_mask
    stacked = jnp.concatenate([jnp.concatenate([real_part, imag_part], axis=4), jnp.concatenate([-imag_part, real_part], axis=4)], axis=3).astype(jnp.bfloat16)
    result = jnp.einsum('acmr,kacrb->kamb', left_factor.astype(jnp.float32), stacked.astype(jnp.float32), preferred_element_type=jnp.float32)
    return result.reshape(batch_count, tile_rows * tile_size, width)


def reference(even_left, even_right, odd_left, odd_right, even_ranks, odd_ranks, even_sources, odd_sources):
    def pick(layer_index, direction):
        pair_index = layer_index // 2
        if layer_index % 2 == 0:
            return even_left[direction, pair_index], even_right[direction, pair_index], even_ranks[direction, pair_index], even_sources[direction, pair_index]
        return odd_left[direction, pair_index], odd_right[direction, pair_index], odd_ranks[direction, pair_index], odd_sources[direction, pair_index]

    down_traces = []
    current = jnp.zeros((NB, NT, 2 * BATCH), jnp.float32)
    for layer_index in range(LAYERS):
        left_factor, right_factor, tile_ranks, sources = pick(layer_index, 0)
        current = tile_product(current.astype(jnp.bfloat16), left_factor, right_factor, tile_ranks) + sources
        down_traces.append(current)
    up_traces = [None] * LAYERS
    current = jnp.zeros((NB, NT, 2 * BATCH), jnp.float32)
    for layer_index in reversed(range(LAYERS)):
        left_factor, right_factor, tile_ranks, sources = pick(layer_index, 1)
        current = tile_product(current.astype(jnp.bfloat16), left_factor, right_factor, tile_ranks) + sources
        up_traces[layer_index] = current
    even_traces = jnp.stack([down_traces[2 * pair_index] + up_traces[2 * pair_index] for pair_index in range(PAIRS)])
    odd_traces = jnp.stack([down_traces[2 * pair_index + 1] + up_traces[2 * pair_index + 1] for pair_index in range(PAIRS)])
    return even_traces, odd_traces
```

```python
import functools

import jax
import jax.numpy as jnp
from jax import lax
from jax.experimental import pallas as pl
from jax.experimental.pallas import tpu as pltpu
from jax.sharding import PartitionSpec as P

MESH = pl.DeviceIdType.MESH


def product_kernel(rows_per, flag_ref, rank_ref, x_ref, v_ref, u_ref, y_ref, xt_ref):
    step = pl.program_id(0)
    cols, tile, twice = v_ref.shape[3], v_ref.shape[4], v_ref.shape[5]
    width = x_ref.shape[1]
    half, batch = twice // 2, width // 2

    @pl.when(flag_ref[0] > 0)
    def _():
        @pl.when(step == 0)
        def _():
            for c in range(cols):
                block = x_ref[c * tile : (c + 1) * tile, :].astype(jnp.float32)
                xt_ref[c] = block.T.astype(jnp.bfloat16)

        lane = lax.broadcasted_iota(jnp.int32, (1, twice), 1)
        sign = jnp.where(lane < half, 1.0, -1.0).astype(jnp.float32)
        within = jnp.where(lane < half, lane, lane - half)
        group = 2 if cols % 2 == 0 else 1
        pair = 2 if rows_per % 2 == 0 else 1
        for a in range(0, rows_per, pair):
            totals = [jnp.zeros((width, tile), jnp.float32) for _ in range(pair)]
            for c in range(0, cols, group):
                stacked = [[None] * group for _ in range(pair)]
                for g in range(group):
                    right = jnp.concatenate([v_ref[0, 0, a + j, c + g] for j in range(pair)], axis=1)
                    coeff = jnp.dot(xt_ref[c + g], right, preferred_element_type=jnp.float32)
                    for j in range(pair):
                        rank = rank_ref[(step * rows_per + a + j) * cols + c + g]
                        mask = (within < rank).astype(jnp.float32)
                        part = coeff[:, j * twice : (j + 1) * twice]
                        top = (part[:batch] * sign - pltpu.roll(part[batch:], half, 1)) * mask
                        low = pltpu.roll(top, half, 1) * (-sign)
                        stacked[j][g] = jnp.concatenate([top, low], axis=0).astype(jnp.bfloat16)
                for j in range(pair):
                    left = jnp.concatenate([u_ref[0, 0, a + j, c + g] for g in range(group)], axis=1)
                    totals[j] += lax.dot_general(
                        jnp.concatenate(stacked[j], axis=1),
                        left,
                        (((1,), (1,)), ((), ())),
                        preferred_element_type=jnp.float32,
                    )
            for j in range(pair):
                y_ref[(a + j) * tile : (a + j + 1) * tile, :] = totals[j].T.astype(y_ref.dtype)


def product(flag, ranks, x, right, left, direction):
    _, _, rows, cols, tile, twice = right.shape
    width = x.shape[1]
    rows_per = 2 if rows % 2 == 0 else 1

    def factor_map(i, flag_ref, rank_ref):
        return (direction, 0, jnp.where(flag_ref[0] > 0, i, 0), 0, 0, 0)

    factor = pl.BlockSpec((1, 1, rows_per, cols, tile, twice), factor_map)
    return pl.pallas_call(
        functools.partial(product_kernel, rows_per),
        out_shape=jax.ShapeDtypeStruct((rows * tile, width), jnp.bfloat16),
        grid_spec=pltpu.PrefetchScalarGridSpec(
            num_scalar_prefetch=2,
            grid=(rows // rows_per,),
            in_specs=[pl.BlockSpec((cols * tile, width), lambda i, f, r: (0, 0)), factor, factor],
            out_specs=pl.BlockSpec((rows_per * tile, width), lambda i, f, r: (i, 0)),
            scratch_shapes=[pltpu.VMEM((cols, width, tile), jnp.bfloat16)],
        ),
        compiler_params=pltpu.CompilerParams(vmem_limit_bytes=40 * 1024 * 1024),
        cost_estimate=pl.CostEstimate(
            flops=4 * rows * cols * tile * twice * width,
            bytes_accessed=4 * rows * cols * tile * twice,
            transcendentals=0,
        ),
        name="tile_product",
    )(flag, ranks, x, right, left)


def peer(axis, offset):
    size = lax.axis_size(axis)
    return lax.rem(lax.axis_index(axis) + offset, size)


def exchange_kernel(spec, *refs):
    step, batches, segments, sides, use_y, edge, last = spec
    refs = list(refs)
    layer = lax.axis_index("layer")
    take = lambda count: [refs.pop(0) for _ in range(count)]
    y_refs = take(2) if use_y else [None, None]
    src_refs = take(2)
    total_refs = take(2)
    x_refs = [None, None] if last else take(2)
    src_bufs, landing = take(2), take(2)
    hand = take(2) if edge and not last else [None, None]
    src_sem, rs_send, rs_recv = take(1)[0], take(2), take(2)
    ag_send, ag_recv = ([None, None], [None, None]) if last else (take(2), take(2))
    shift_send, shift_recv = take(2) if edge and not last else (None, None)

    plan = []
    for side in range(2):
        direction, rs_axis, ag_axis = sides[side]
        distance = layer if direction > 0 else segments - 1 - layer
        slot = step - distance
        active = (slot >= 0) & (slot < batches)
        have_y = active if edge else active & (distance > 0)
        sends = active & (distance < segments - 1)
        receives = (slot + 1 >= 0) & (slot + 1 < batches) & (distance > 0)
        plan.append((direction, rs_axis, ag_axis, slot, active, have_y, sends, receives))

    barrier = pltpu.get_barrier_semaphore()
    expect = 0
    for axis in ("row", "col"):
        for k in range(1, lax.axis_size(axis)):
            pl.semaphore_signal(
                barrier, inc=1, device_id={axis: peer(axis, k)}, device_id_type=MESH
            )
            expect += 1
    expect = jnp.int32(expect)
    if edge and not last:
        for direction, _, _, _, _, _, sends, receives in plan:

            @pl.when(receives)
            def _(direction=direction):
                pl.semaphore_signal(
                    barrier, inc=1, device_id={"layer": layer - direction}, device_id_type=MESH
                )

            expect = expect + jnp.where(sends, 1, 0)

    def source_copy(side):
        slot = plan[side][3]
        direction = 0 if plan[side][0] > 0 else 1
        return pltpu.make_async_copy(
            src_refs[side].at[direction, 0, slot], src_bufs[side], src_sem.at[side]
        )

    for side in range(2):

        @pl.when(plan[side][4])
        def _(side=side):
            source_copy(side).start()

    pl.semaphore_wait(barrier, expect)
    shard = src_bufs[0].shape[0]

    def rs_copy(side, k):
        target = peer(plan[side][1], k)
        return pltpu.make_async_remote_copy(
            src_ref=y_refs[side].at[pl.ds(pl.multiple_of(target * shard, shard), shard)],
            dst_ref=landing[side].at[k - 1],
            send_sem=rs_send[side].at[k - 1],
            recv_sem=rs_recv[side].at[k - 1],
            device_id={plan[side][1]: target},
            device_id_type=MESH,
        )

    def ag_own(side):
        own = lax.axis_index(plan[side][2])
        return x_refs[side].at[pl.ds(pl.multiple_of(own * shard, shard), shard)]

    def ag_copy(side, k):
        return pltpu.make_async_remote_copy(
            src_ref=ag_own(side),
            dst_ref=ag_own(side),
            send_sem=ag_send[side].at[k - 1],
            recv_sem=ag_recv[side].at[k - 1],
            device_id={plan[side][2]: peer(plan[side][2], k)},
            device_id_type=MESH,
        )

    def shift_copy(side):
        return pltpu.make_async_remote_copy(
            src_ref=hand[side],
            dst_ref=ag_own(side),
            send_sem=shift_send.at[side],
            recv_sem=shift_recv.at[side],
            device_id={"layer": layer + plan[side][0]},
            device_id_type=MESH,
        )

    def peers(axis):
        return range(1, lax.axis_size(axis))

    order = sorted(range(2), key=lambda side: 0 if sides[side][1] == "row" else 1)
    for side in order:
        if use_y:

            @pl.when(plan[side][5])
            def _(side=side):
                for k in peers(plan[side][1]):
                    rs_copy(side, k).start()

    for side in order:
        direction, rs_axis, ag_axis, slot, active, have_y, sends, receives = plan[side]

        @pl.when(active)
        def _(side=side):
            source_copy(side).wait()

        if use_y:

            @pl.when(have_y)
            def _(side=side, rs_axis=rs_axis):
                for k in peers(rs_axis):
                    rs_copy(side, k).wait_recv()
                own = pl.multiple_of(lax.axis_index(rs_axis) * shard, shard)
                value = src_bufs[side][...] + y_refs[side][pl.ds(own, shard), :].astype(jnp.float32)
                for k in peers(rs_axis):
                    value = value + landing[side][k - 1].astype(jnp.float32)
                total_refs[side][...] = value

            plain = active & jnp.logical_not(have_y)
        else:
            plain = active
        if not edge:

            @pl.when(plain)
            def _(side=side):
                total_refs[side][...] = src_bufs[side][...]

            @pl.when(active)
            def _(side=side, ag_axis=ag_axis):
                own = pl.multiple_of(lax.axis_index(ag_axis) * shard, shard)
                x_refs[side][pl.ds(own, shard), :] = total_refs[side][...].astype(jnp.bfloat16)
                for k in peers(ag_axis):
                    ag_copy(side, k).start()

        elif not last:

            @pl.when(sends)
            def _(side=side):
                hand[side][...] = total_refs[side][...].astype(jnp.bfloat16)
                shift_copy(side).start()

    if edge and not last:
        for side in order:

            @pl.when(plan[side][7])
            def _(side=side):
                shift_copy(side).wait_recv()
                for k in peers(plan[side][2]):
                    ag_copy(side, k).start()

    for side in order:
        if use_y:

            @pl.when(plan[side][5])
            def _(side=side):
                for k in peers(plan[side][1]):
                    rs_copy(side, k).wait_send()

        if last:
            continue
        if edge:

            @pl.when(plan[side][6])
            def _(side=side):
                shift_copy(side).wait_send()

        @pl.when(plan[side][7] if edge else plan[side][4])
        def _(side=side):
            for k in peers(plan[side][2]):
                ag_copy(side, k).wait()


def exchange(step, edge, last, y_pair, src_pair, collective_id):
    batches = src_pair[0].shape[2]
    shard, width = src_pair[0].shape[3:]
    segments = lax.axis_size("layer")
    if edge:
        sides = ((1, "row", "row"), (-1, "col", "col"))
    else:
        sides = ((1, "col", "col"), (-1, "row", "row"))
    use_y = y_pair is not None
    spec = (step, batches, segments, sides, use_y, edge, last)
    operands = (list(y_pair) if use_y else []) + list(src_pair)
    vmem = pl.BlockSpec(memory_space=pltpu.VMEM)
    anywhere = pl.BlockSpec(memory_space=pl.ANY)
    in_specs = ([vmem] * 2 if use_y else []) + [anywhere] * 2
    outs = [jax.ShapeDtypeStruct((shard, width), jnp.float32)] * 2
    if not last:
        outs += [
            jax.ShapeDtypeStruct((lax.axis_size(side[2]) * shard, width), jnp.bfloat16)
            for side in sides
        ]
    count = [max(lax.axis_size(side[1]) - 1, 1) for side in sides]
    scratch = [pltpu.VMEM((shard, width), jnp.float32)] * 2
    scratch += [pltpu.VMEM((n, shard, width), jnp.bfloat16) for n in count]
    if edge and not last:
        scratch += [pltpu.VMEM((shard, width), jnp.bfloat16)] * 2
    scratch += [pltpu.SemaphoreType.DMA((2,))]
    scratch += [pltpu.SemaphoreType.DMA((n,)) for n in count] * 2
    if not last:
        scratch += [pltpu.SemaphoreType.DMA((n,)) for n in count] * 2
    if edge and not last:
        scratch += [pltpu.SemaphoreType.DMA((2,))] * 2
    return pl.pallas_call(
        functools.partial(exchange_kernel, spec),
        out_shape=outs,
        in_specs=in_specs,
        out_specs=[vmem] * len(outs),
        scratch_shapes=scratch,
        compiler_params=pltpu.CompilerParams(
            collective_id=collective_id,
            has_side_effects=True,
            vmem_limit_bytes=40 * 1024 * 1024,
        ),
        name="exchange_edge" if edge else "exchange_mid",
    )(*operands)


def on_device(
    even_left, even_right, odd_left, odd_right, even_ranks, odd_ranks, even_sources, odd_sources
):
    segments = lax.axis_size("layer")
    layer = lax.axis_index("layer")
    batches = even_sources.shape[2]
    even_flat = [even_ranks[e, 0].reshape(-1) for e in range(2)]
    odd_flat = [odd_ranks[e, 0].reshape(-1) for e in range(2)]

    def flag(slot, skip):
        active = (slot >= 0) & (slot < batches) & jnp.logical_not(skip)
        return active.astype(jnp.int32).reshape(1)

    never = jnp.bool_(False)
    history = []
    x_down = x_up = None
    total_steps = batches + segments - 1
    for step in range(total_steps):
        down_slot = step - layer
        up_slot = step - (segments - 1 - layer)
        last = step + 1 == total_steps
        if step == 0:
            y_pair = None
        else:
            y_pair = (
                product(
                    flag(down_slot, layer == 0), even_flat[0], x_down, even_right, even_left, 0
                ),
                product(
                    flag(up_slot, layer == segments - 1), odd_flat[1], x_up, odd_right, odd_left, 1
                ),
            )
        down_even, up_odd, x_down, x_up = exchange(
            step, False, False, y_pair, (even_sources, odd_sources), 2 * step
        )
        y_pair = (
            product(flag(down_slot, never), odd_flat[0], x_down, odd_right, odd_left, 0),
            product(flag(up_slot, never), even_flat[1], x_up, even_right, even_left, 1),
        )
        result = exchange(step, True, last, y_pair, (odd_sources, even_sources), 2 * step + 1)
        down_odd, up_even = result[:2]
        if not last:
            x_down, x_up = result[2:]
        history.append((down_even, down_odd, up_even, up_odd))

    def chosen(which, batch, distance):
        picked = history[batch][which]
        for away in range(1, segments):
            picked = jnp.where(distance == away, history[batch + away][which], picked)
        return picked

    up_distance = segments - 1 - layer
    even_traces = jnp.stack(
        [chosen(0, m, layer) + chosen(2, m, up_distance) for m in range(batches)]
    )[None]
    odd_traces = jnp.stack(
        [chosen(1, m, layer) + chosen(3, m, up_distance) for m in range(batches)]
    )[None]
    return (even_traces, odd_traces)


def solution(mesh):
    in_specs = (
        P(None, "layer", "row", "col", None, None),
        P(None, "layer", "row", "col", None, None),
        P(None, "layer", "col", "row", None, None),
        P(None, "layer", "col", "row", None, None),
        P(None, "layer", "row", "col"),
        P(None, "layer", "col", "row"),
        P(None, "layer", None, ("row", "col"), None),
        P(None, "layer", None, ("col", "row"), None),
    )
    out_specs = (P("layer", None, ("row", "col"), None), P("layer", None, ("col", "row"), None))
    return jax.shard_map(
        on_device, mesh=mesh, in_specs=in_specs, out_specs=out_specs, check_vma=False
    )
```

```python
import functools

import jax
import jax.numpy as jnp
from jax import lax
from jax.experimental import pallas as pl
from jax.experimental.pallas import tpu as pltpu
from jax.sharding import PartitionSpec as P

MESH = pl.DeviceIdType.MESH


def product_kernel(rows_per, flag_ref, rank_ref, x_ref, v_ref, u_ref, y_ref, xt_ref):
    step = pl.program_id(0)
    cols, tile, twice = v_ref.shape[3], v_ref.shape[4], v_ref.shape[5]
    width = x_ref.shape[1]
    half, batch = twice // 2, width // 2

    @pl.when(flag_ref[0] > 0)
    def _():
        @pl.when(step == 0)
        def _():
            for c in range(cols):
                block = x_ref[c * tile : (c + 1) * tile, :].astype(jnp.float32)
                xt_ref[c] = block.T.astype(jnp.bfloat16)

        lane = lax.broadcasted_iota(jnp.int32, (1, twice), 1)
        sign = jnp.where(lane < half, 1.0, -1.0).astype(jnp.float32)
        within = jnp.where(lane < half, lane, lane - half)
        group = 2 if cols % 2 == 0 else 1
        pair = 2 if rows_per % 2 == 0 else 1
        for a in range(0, rows_per, pair):
            totals = [jnp.zeros((width, tile), jnp.float32) for _ in range(pair)]
            for c in range(0, cols, group):
                stacked = [[None] * group for _ in range(pair)]
                for g in range(group):
                    right = jnp.concatenate([v_ref[0, 0, a + j, c + g] for j in range(pair)], axis=1)
                    coeff = jnp.dot(xt_ref[c + g], right, preferred_element_type=jnp.float32)
                    for j in range(pair):
                        rank = rank_ref[(step * rows_per + a + j) * cols + c + g]
                        mask = (within < rank).astype(jnp.float32)
                        part = coeff[:, j * twice : (j + 1) * twice]
                        top = (part[:batch] * sign - pltpu.roll(part[batch:], half, 1)) * mask
                        low = pltpu.roll(top, half, 1) * (-sign)
                        stacked[j][g] = jnp.concatenate([top, low], axis=0).astype(jnp.bfloat16)
                for j in range(pair):
                    left = jnp.concatenate([u_ref[0, 0, a + j, c + g] for g in range(group)], axis=1)
                    totals[j] += lax.dot_general(
                        jnp.concatenate(stacked[j], axis=1),
                        left,
                        (((1,), (1,)), ((), ())),
                        preferred_element_type=jnp.float32,
                    )
            for j in range(pair):
                y_ref[(a + j) * tile : (a + j + 1) * tile, :] = totals[j].T.astype(y_ref.dtype)


def product(flag, ranks, x, right, left, direction):
    _, _, rows, cols, tile, twice = right.shape
    width = x.shape[1]
    rows_per = 2 if rows % 2 == 0 else 1

    def factor_map(i, flag_ref, rank_ref):
        return (direction, 0, jnp.where(flag_ref[0] > 0, i, 0), 0, 0, 0)

    factor = pl.BlockSpec((1, 1, rows_per, cols, tile, twice), factor_map)
    return pl.pallas_call(
        functools.partial(product_kernel, rows_per),
        out_shape=jax.ShapeDtypeStruct((rows * tile, width), jnp.bfloat16),
        grid_spec=pltpu.PrefetchScalarGridSpec(
            num_scalar_prefetch=2,
            grid=(rows // rows_per,),
            in_specs=[pl.BlockSpec(memory_space=pltpu.VMEM), factor, factor],
            out_specs=pl.BlockSpec((rows_per * tile, width), lambda i, f, r: (i, 0)),
            scratch_shapes=[pltpu.VMEM((cols, width, tile), jnp.bfloat16)],
        ),
        compiler_params=pltpu.CompilerParams(vmem_limit_bytes=50 * 1024 * 1024),
        cost_estimate=pl.CostEstimate(
            flops=4 * rows * cols * tile * twice * width,
            bytes_accessed=4 * rows * cols * tile * twice,
            transcendentals=0,
        ),
        name="tile_product",
    )(flag, ranks, x, right, left)


def peer(axis, offset):
    size = lax.axis_size(axis)
    return lax.rem(lax.axis_index(axis) + offset, size)


def exchange_kernel(spec, *refs):
    step, batches, segments, sides, use_y, edge, last = spec
    refs = list(refs)
    layer = lax.axis_index("layer")
    take = lambda count: [refs.pop(0) for _ in range(count)]
    y_refs = take(2) if use_y else [None, None]
    src_refs = take(2)
    total_outs = take(2)
    x_refs = [None, None] if last else take(2)
    src_bufs, landing, total_refs = take(2), take(2), take(2)
    out_sem = take(1)[0]
    hand = take(2) if edge and not last else [None, None]
    src_sem, rs_send, rs_recv = take(1)[0], take(2), take(2)
    ag_send, ag_recv = ([None, None], [None, None]) if last else (take(2), take(2))
    shift_send, shift_recv = take(2) if edge and not last else (None, None)

    plan = []
    for side in range(2):
        direction, rs_axis, ag_axis = sides[side]
        distance = layer if direction > 0 else segments - 1 - layer
        slot = step - distance
        active = (slot >= 0) & (slot < batches)
        have_y = active if edge else active & (distance > 0)
        sends = active & (distance < segments - 1)
        receives = (slot + 1 >= 0) & (slot + 1 < batches) & (distance > 0)
        plan.append((direction, rs_axis, ag_axis, slot, active, have_y, sends, receives))

    barrier = pltpu.get_barrier_semaphore()
    expect = 0
    for axis in ("row", "col"):
        for k in range(1, lax.axis_size(axis)):
            pl.semaphore_signal(
                barrier, inc=1, device_id={axis: peer(axis, k)}, device_id_type=MESH
            )
            expect += 1
    expect = jnp.int32(expect)
    if edge and not last:
        for direction, _, _, _, _, _, sends, receives in plan:

            @pl.when(receives)
            def _(direction=direction):
                pl.semaphore_signal(
                    barrier, inc=1, device_id={"layer": layer - direction}, device_id_type=MESH
                )

            expect = expect + jnp.where(sends, 1, 0)

    def total_copy(side):
        return pltpu.make_async_copy(total_refs[side], total_outs[side], out_sem.at[side])

    def source_copy(side):
        slot = plan[side][3]
        direction = 0 if plan[side][0] > 0 else 1
        return pltpu.make_async_copy(
            src_refs[side].at[direction, 0, slot], src_bufs[side], src_sem.at[side]
        )

    for side in range(2):

        @pl.when(plan[side][4])
        def _(side=side):
            source_copy(side).start()

    pl.semaphore_wait(barrier, expect)
    shard = src_bufs[0].shape[0]

    def rs_copy(side, k):
        target = peer(plan[side][1], k)
        return pltpu.make_async_remote_copy(
            src_ref=y_refs[side].at[pl.ds(pl.multiple_of(target * shard, shard), shard)],
            dst_ref=landing[side].at[k - 1],
            send_sem=rs_send[side].at[k - 1],
            recv_sem=rs_recv[side].at[k - 1],
            device_id={plan[side][1]: target},
            device_id_type=MESH,
        )

    def ag_own(side):
        own = lax.axis_index(plan[side][2])
        return x_refs[side].at[pl.ds(pl.multiple_of(own * shard, shard), shard)]

    def ag_copy(side, k):
        return pltpu.make_async_remote_copy(
            src_ref=ag_own(side),
            dst_ref=ag_own(side),
            send_sem=ag_send[side].at[k - 1],
            recv_sem=ag_recv[side].at[k - 1],
            device_id={plan[side][2]: peer(plan[side][2], k)},
            device_id_type=MESH,
        )

    def shift_copy(side):
        return pltpu.make_async_remote_copy(
            src_ref=hand[side],
            dst_ref=ag_own(side),
            send_sem=shift_send.at[side],
            recv_sem=shift_recv.at[side],
            device_id={"layer": layer + plan[side][0]},
            device_id_type=MESH,
        )

    def peers(axis):
        return range(1, lax.axis_size(axis))

    order = sorted(range(2), key=lambda side: 0 if sides[side][1] == "row" else 1)
    for side in order:
        if use_y:

            @pl.when(plan[side][5])
            def _(side=side):
                for k in peers(plan[side][1]):
                    rs_copy(side, k).start()

    for side in order:
        direction, rs_axis, ag_axis, slot, active, have_y, sends, receives = plan[side]

        @pl.when(active)
        def _(side=side):
            source_copy(side).wait()

        if use_y:

            @pl.when(have_y)
            def _(side=side, rs_axis=rs_axis):
                for k in peers(rs_axis):
                    rs_copy(side, k).wait_recv()
                own = pl.multiple_of(lax.axis_index(rs_axis) * shard, shard)
                value = src_bufs[side][...] + y_refs[side][pl.ds(own, shard), :].astype(jnp.float32)
                for k in peers(rs_axis):
                    value = value + landing[side][k - 1].astype(jnp.float32)
                total_refs[side][...] = value

            plain = active & jnp.logical_not(have_y)
        else:
            plain = active
        if edge:

            @pl.when(active)
            def _(side=side):
                total_copy(side).start()

        else:

            @pl.when(plain)
            def _(side=side):
                total_refs[side][...] = src_bufs[side][...]

            @pl.when(active)
            def _(side=side, ag_axis=ag_axis):
                total_copy(side).start()
                own = pl.multiple_of(lax.axis_index(ag_axis) * shard, shard)
                x_refs[side][pl.ds(own, shard), :] = total_refs[side][...].astype(jnp.bfloat16)
                for k in peers(ag_axis):
                    ag_copy(side, k).start()

        if edge and not last:

            @pl.when(sends)
            def _(side=side):
                hand[side][...] = total_refs[side][...].astype(jnp.bfloat16)
                shift_copy(side).start()

    if edge and not last:
        for side in order:

            @pl.when(plan[side][7])
            def _(side=side):
                shift_copy(side).wait_recv()
                for k in peers(plan[side][2]):
                    ag_copy(side, k).start()

    for side in order:

        @pl.when(plan[side][4])
        def _(side=side):
            total_copy(side).wait()

        if use_y:

            @pl.when(plan[side][5])
            def _(side=side):
                for k in peers(plan[side][1]):
                    rs_copy(side, k).wait_send()

        if last:
            continue
        if edge:

            @pl.when(plan[side][6])
            def _(side=side):
                shift_copy(side).wait_send()

        @pl.when(plan[side][7] if edge else plan[side][4])
        def _(side=side):
            for k in peers(plan[side][2]):
                ag_copy(side, k).wait()


def exchange(step, edge, last, y_pair, src_pair, collective_id):
    batches = src_pair[0].shape[2]
    shard, width = src_pair[0].shape[3:]
    segments = lax.axis_size("layer")
    if edge:
        sides = ((1, "row", "row"), (-1, "col", "col"))
    else:
        sides = ((1, "col", "col"), (-1, "row", "row"))
    use_y = y_pair is not None
    spec = (step, batches, segments, sides, use_y, edge, last)
    operands = (list(y_pair) if use_y else []) + list(src_pair)
    vmem = pl.BlockSpec(memory_space=pltpu.VMEM)
    anywhere = pl.BlockSpec(memory_space=pltpu.HBM)
    in_specs = ([vmem] * 2 if use_y else []) + [anywhere] * 2
    outs = [jax.ShapeDtypeStruct((shard, width), jnp.float32)] * 2
    if not last:
        outs += [
            jax.ShapeDtypeStruct((lax.axis_size(side[2]) * shard, width), jnp.bfloat16)
            for side in sides
        ]
    count = [max(lax.axis_size(side[1]) - 1, 1) for side in sides]
    scratch = [pltpu.VMEM((shard, width), jnp.float32)] * 2
    scratch += [pltpu.VMEM((n, shard, width), jnp.bfloat16) for n in count]
    scratch += [pltpu.VMEM((shard, width), jnp.float32)] * 2
    scratch += [pltpu.SemaphoreType.DMA((2,))]
    if edge and not last:
        scratch += [pltpu.VMEM((shard, width), jnp.bfloat16)] * 2
    scratch += [pltpu.SemaphoreType.DMA((2,))]
    scratch += [pltpu.SemaphoreType.DMA((n,)) for n in count] * 2
    if not last:
        scratch += [pltpu.SemaphoreType.DMA((n,)) for n in count] * 2
    if edge and not last:
        scratch += [pltpu.SemaphoreType.DMA((2,))] * 2
    return pl.pallas_call(
        functools.partial(exchange_kernel, spec),
        out_shape=outs,
        in_specs=in_specs,
        out_specs=[anywhere] * 2 + [vmem] * (len(outs) - 2),
        scratch_shapes=scratch,
        compiler_params=pltpu.CompilerParams(
            collective_id=collective_id,
            has_side_effects=True,
            vmem_limit_bytes=50 * 1024 * 1024,
        ),
        name="exchange_edge" if edge else "exchange_mid",
    )(*operands)


def on_device(
    even_left, even_right, odd_left, odd_right, even_ranks, odd_ranks, even_sources, odd_sources
):
    segments = lax.axis_size("layer")
    layer = lax.axis_index("layer")
    batches = even_sources.shape[2]
    even_flat = [even_ranks[e, 0].reshape(-1) for e in range(2)]
    odd_flat = [odd_ranks[e, 0].reshape(-1) for e in range(2)]

    def flag(slot, skip):
        active = (slot >= 0) & (slot < batches) & jnp.logical_not(skip)
        return active.astype(jnp.int32).reshape(1)

    never = jnp.bool_(False)
    history = []
    x_down = x_up = None
    total_steps = batches + segments - 1
    for step in range(total_steps):
        down_slot = step - layer
        up_slot = step - (segments - 1 - layer)
        last = step + 1 == total_steps
        if step == 0:
            y_pair = None
        else:
            y_pair = (
                product(
                    flag(down_slot, layer == 0), even_flat[0], x_down, even_right, even_left, 0
                ),
                product(
                    flag(up_slot, layer == segments - 1), odd_flat[1], x_up, odd_right, odd_left, 1
                ),
            )
        down_even, up_odd, x_down, x_up = exchange(
            step, False, False, y_pair, (even_sources, odd_sources), 2 * step
        )
        y_pair = (
            product(flag(down_slot, never), odd_flat[0], x_down, odd_right, odd_left, 0),
            product(flag(up_slot, never), even_flat[1], x_up, even_right, even_left, 1),
        )
        result = exchange(step, True, last, y_pair, (odd_sources, even_sources), 2 * step + 1)
        down_odd, up_even = result[:2]
        if not last:
            x_down, x_up = result[2:]
        history.append((down_even, down_odd, up_even, up_odd))

    def chosen(which, batch, distance):
        picked = history[batch][which]
        for away in range(1, segments):
            picked = jnp.where(distance == away, history[batch + away][which], picked)
        return picked

    up_distance = segments - 1 - layer
    even_traces = jnp.stack(
        [chosen(0, m, layer) + chosen(2, m, up_distance) for m in range(batches)]
    )[None]
    odd_traces = jnp.stack(
        [chosen(1, m, layer) + chosen(3, m, up_distance) for m in range(batches)]
    )[None]
    return (even_traces, odd_traces)


def solution(mesh):
    in_specs = (
        P(None, "layer", "row", "col", None, None),
        P(None, "layer", "row", "col", None, None),
        P(None, "layer", "col", "row", None, None),
        P(None, "layer", "col", "row", None, None),
        P(None, "layer", "row", "col"),
        P(None, "layer", "col", "row"),
        P(None, "layer", None, ("row", "col"), None),
        P(None, "layer", None, ("col", "row"), None),
    )
    out_specs = (P("layer", None, ("row", "col"), None), P("layer", None, ("col", "row"), None))
    return jax.shard_map(
        on_device, mesh=mesh, in_specs=in_specs, out_specs=out_specs, check_vma=False
    )
```
